32 devices in a mesh: sect: 4 (over x, core), cell: 8 (over z, y).
Axes of the slice: x: 2, y: 2, z: 4, core: 2. Of those that a mesh axis runs over, the one named last changes fastest.
Arguments:
- atm_fields: bfloat16 [24, 131072], P(None, ('sect', 'cell')), may hold values from -6 to 6
- ocn_state: float32 [8, 262144], P(None, ('sect', 'cell')), may hold values from -6 to 6
- ice_state: float32 [8, 262144], P(None, ('sect', 'cell')), may hold values from -6 to 6
- ice_level: int32 [262144], P(('sect', 'cell')), may hold values from 0 to 8
- lnd_state: float32 [8, 65536], P(None, ('sect', 'cell')), may hold values from -6 to 6
- lnd_level: int32 [65536], P(('sect', 'cell')), may hold values from 1 to 8
- ocn_map: int32 [2048, 2], P(('sect', 'cell')), may hold values from 0 to 1023, as said below
- ocn_local: int32 [2048, 2], P(('sect', 'cell')), may hold values from 0 to 31
- ocn_tiles: bfloat16 [2048, 4, 128, 128], P(('sect', 'cell')), may hold values from -0.25 to 0.25
- lnd_map: int32 [512, 2], P(('sect', 'cell')), may hold values from 0 to 1023, as said below
- lnd_local: int32 [512, 2], P(('sect', 'cell')), may hold values from 0 to 31
- lnd_tiles: bfloat16 [512, 4, 128, 128], P(('sect', 'cell')), may hold values from -0.25 to 0.25
Outputs:
- atm_flux: float32 [8, 131072], P(None, ('sect', 'cell'))
- ocn_flux: float32 [8, 262144], P(None, ('sect', 'cell'))
- lnd_flux: float32 [8, 65536], P(None, ('sect', 'cell'))
The draws below stay inside these ranges and needn't reach their ends.
Inputs may be any that keep to these rules, and one draw needn't show every extreme that they name: Global atmosphere block indices; the device of block b is b // 32, and devices are numbered sect-major. For the ocn_map rows of one device q's 64 ocean blocks taken together with the lnd_map rows of its 16 land blocks, every named device is (q + t) modulo the device count for some t from -4 to 3; at most 30 of these entries name any one device, and exactly 30 name some device. `lnd_map`: global atmosphere block indices, counted together with ocn_map as stated there.
All inputs are finite; a program needn't handle non-finite values.
Results may differ from the reference program's by a relative error of at most 0.0022.
Values may be sent and summed in bfloat16 or wider, within the bound.
A program may use at most 64 MiB of HBM per device.

```python
import jax
import jax.numpy as jnp
from jax import lax

FIELDS = 24
FLUXES = 8
BLOCK = 128
KR = 2
KL = 2
AB_DEV = 32
OB_DEV = 64
LB_DEV = 16
C_PEER = 30
NAB = 1024
NA = 131072
NOB = 2048
NO = 262144
NLB = 512
NL = 65536
N_SECT = 4
N_CELL = 8


def remote_sources(key):
    key = jax.random.fold_in(key, 7)
    device_count = NAB // AB_DEV
    pair_count = (OB_DEV + LB_DEV) * KR
    window = N_CELL
    offsets = jnp.arange(window, dtype=jnp.int32) - window // 2
    copies = window * C_PEER

    def draw_device(subkey, device):
        key_heavy, key_score, key_order, key_local = jax.random.split(subkey, 4)
        heavy = jax.random.randint(key_heavy, (), 0, window).astype(jnp.int32)
        peer = jnp.repeat(jnp.arange(window, dtype=jnp.int32), C_PEER)
        noise = jax.random.randint(key_score, (copies,), 0, 3 * window).astype(jnp.int32)
        score = noise + 2 * jnp.abs(offsets[peer])
        score = jnp.where(peer == heavy, -1, score)
        keyed = (score + 1) * copies + jnp.arange(copies, dtype=jnp.int32)
        chosen = peer[jnp.argsort(keyed)[:pair_count]]
        owners = (device + offsets[chosen]) % device_count
        owners = jax.random.permutation(key_order, owners).astype(jnp.int32)
        local_block = jax.random.randint(key_local, (pair_count,), 0, AB_DEV).astype(jnp.int32)
        return (owners * AB_DEV + local_block).astype(jnp.int32)
    keys = jax.random.split(key, device_count)
    return jax.vmap(draw_device)(keys, jnp.arange(device_count, dtype=jnp.int32))


def draw_ocn_map(key, part):
    source_table = remote_sources(key)
    return source_table[:, :OB_DEV * KR].reshape(-1, KR)


def draw_lnd_map(key, part):
    source_table = remote_sources(key)
    return source_table[:, OB_DEV * KR:].reshape(-1, KR)


def set_ends(entries, rng, least, top_value):
    index_at = [jax.random.randint(jax.random.fold_in(rng, axis), (), 0, length) for axis, length in enumerate(entries.shape)]
    main_axis = entries.shape.index(max(entries.shape))
    next_to = index_at[:main_axis] + [(index_at[main_axis] + 1) % entries.shape[main_axis]] + index_at[main_axis + 1:]
    return entries.at[tuple(index_at)].set(least).at[tuple(next_to)].set(top_value)


def block_levels(key, dims, shards, low, top_value):
    def one(dim, shards_of):
        steps = jax.random.uniform(jax.random.fold_in(jax.random.fold_in(key, 6), dim), (shards_of,), jnp.float32, low / len(shards), top_value / len(shards))
        return jnp.repeat(jnp.exp(steps), dims[dim] // shards_of).reshape((-1,) + (1,) * (len(dims) - dim - 1))

    factor_of = one(*shards[0])
    for cut in shards[1:]:
        factor_of = factor_of * one(*cut)
    return factor_of


def normal_values(stream_key, extent, width, most, cuts=(), kind=jnp.bfloat16):
    drawn = width * jax.random.normal(stream_key, extent, jnp.float32)
    if cuts:
        drawn = drawn * block_levels(stream_key, extent, cuts, -0.22, 0.18)
    return jnp.clip(drawn, -most, most).astype(kind)


def setup_inputs(seed: int = 0) -> dict:
    seeds = jax.random.split(jax.random.key(seed), 13)
    atm_fields = normal_values(seeds[0], (FIELDS, NA), 1.0, 6.0, ((1, 32),))
    ocn_state = normal_values(seeds[1], (FLUXES, NO), 1.0, 6.0, ((1, 32),), jnp.float32)
    ice_state = normal_values(seeds[2], (FLUXES, NO), 1.0, 6.0, ((1, 32),), jnp.float32)
    ice_level = set_ends(jax.random.randint(seeds[3], (NO,), 0, 9), jax.random.fold_in(seeds[3], 1), 0, 8).astype(jnp.int32)
    lnd_state = normal_values(seeds[4], (FLUXES, NL), 1.0, 6.0, ((1, 32),), jnp.float32)
    lnd_level = set_ends(jax.random.randint(seeds[5], (NL,), 1, 9), jax.random.fold_in(seeds[5], 1), 1, 8).astype(jnp.int32)
    ocn_map = draw_ocn_map(jax.random.fold_in(seeds[12], 71), 0)
    ocn_local = set_ends(jax.random.randint(seeds[7], (NOB, KL), 0, AB_DEV), jax.random.fold_in(seeds[7], 1), 0, AB_DEV - 1).astype(jnp.int32)
    ocn_tiles = normal_values(seeds[8], (NOB, KR + KL, BLOCK, BLOCK), (BLOCK * (KR + KL)) ** -0.5, 0.25, ((0, 32),))
    lnd_map = draw_lnd_map(jax.random.fold_in(seeds[12], 71), 0)
    lnd_local = set_ends(jax.random.randint(seeds[10], (NLB, KL), 0, AB_DEV), jax.random.fold_in(seeds[10], 1), 0, AB_DEV - 1).astype(jnp.int32)
    lnd_tiles = normal_values(seeds[11], (NLB, KR + KL, BLOCK, BLOCK), (BLOCK * (KR + KL)) ** -0.5, 0.25, ((0, 32),))
    return {"atm_fields": atm_fields, "ocn_state": ocn_state, "ice_state": ice_state, "ice_level": ice_level, "lnd_state": lnd_state, "lnd_level": lnd_level, "ocn_map": ocn_map, "ocn_local": ocn_local, "ocn_tiles": ocn_tiles, "lnd_map": lnd_map, "lnd_local": lnd_local, "lnd_tiles": lnd_tiles}


ocean_coef = (1.2, 0.9, 1.5, 0.7, 1.1, 1.3, 0.8, 1.0)
ice_coef = (0.5, 1.4, 0.6, 1.2, 0.9, 0.4, 1.6, 0.7)
land_coef = (0.8, 1.1, 0.6, 1.5, 0.7, 1.2, 1.0, 0.5)

def bulk_flux(remapped, surface, factors):
    wind_speed = jnp.sqrt(1.0 + remapped[:, 0::3] * remapped[:, 0::3] + remapped[:, 1::3] * remapped[:, 1::3])
    weights = jnp.asarray(factors, jnp.float32)[None, :, None]
    return weights * wind_speed * (remapped[:, 2::3] - surface)

def to_blocks(array, count):
    return array.reshape(array.shape[0], count, BLOCK).transpose(1, 0, 2)

def remap_forward(atm_blocks, remote_map, local_map, tiles, device_count, per_device):
    offsets = (jnp.arange(device_count, dtype=jnp.int32) * AB_DEV)[:, None, None]
    remote_ids = remote_map.reshape(device_count, per_device, KR).astype(jnp.int32)
    local_ids = local_map.reshape(device_count, per_device, KL).astype(jnp.int32) + offsets
    targets = jnp.concatenate([remote_ids, local_ids], axis=2)
    tile_sets = tiles.reshape(device_count, per_device, KR + KL, BLOCK, BLOCK)

    def forward(operand):
        indices, tile_set = operand
        sources = atm_blocks[indices].astype(jnp.float32)
        return jnp.einsum('bkfs,bksd->bfd', sources, tile_set.astype(jnp.float32))
    mixed = lax.map(forward, (targets, tile_sets))
    return (targets, mixed.reshape(device_count * per_device, FIELDS, BLOCK))

def remap_back(flux, tiles, device_count, per_device):
    rounded = flux.astype(jnp.bfloat16).reshape(device_count, per_device, FLUXES, BLOCK)
    tile_sets = tiles.reshape(device_count, per_device, KR + KL, BLOCK, BLOCK)

    def backward(operand):
        flux_set, tile_set = operand
        return jnp.einsum('bfd,bksd->bkfs', flux_set.astype(jnp.float32), tile_set.astype(jnp.float32))
    terms = lax.map(backward, (rounded, tile_sets))
    return terms.reshape(-1, FLUXES * BLOCK)

def reference(atm_fields, ocn_state, ice_state, ice_level, lnd_state, lnd_level, ocn_map, ocn_local, ocn_tiles, lnd_map, lnd_local, lnd_tiles):
    device_count = N_SECT * N_CELL
    atm_blocks = to_blocks(atm_fields, NAB)
    ocean_targets, ocean_mixed = remap_forward(atm_blocks, ocn_map, ocn_local, ocn_tiles, device_count, OB_DEV)
    land_targets, land_mixed = remap_forward(atm_blocks, lnd_map, lnd_local, lnd_tiles, device_count, LB_DEV)
    ice_frac = (ice_level.astype(jnp.float32) / 8.0).reshape(NOB, 1, BLOCK)
    ocean_flux = (1.0 - ice_frac) * bulk_flux(ocean_mixed, to_blocks(ocn_state, NOB), ocean_coef) + ice_frac * bulk_flux(ocean_mixed, to_blocks(ice_state, NOB), ice_coef)
    land_frac = (lnd_level.astype(jnp.float32) / 8.0).reshape(NLB, 1, BLOCK)
    land_flux = land_frac * bulk_flux(land_mixed, to_blocks(lnd_state, NLB), land_coef)
    ocean_terms = remap_back(ocean_flux, ocn_tiles, device_count, OB_DEV)
    land_terms = remap_back(land_flux, lnd_tiles, device_count, LB_DEV)
    summed = jax.ops.segment_sum(ocean_terms, ocean_targets.reshape(-1), num_segments=NAB)
    summed = summed + jax.ops.segment_sum(land_terms, land_targets.reshape(-1), num_segments=NAB)
    atm_flux = summed.reshape(NAB, FLUXES, BLOCK).transpose(1, 0, 2).reshape(FLUXES, NA)
    ocn_flux = ocean_flux.transpose(1, 0, 2).reshape(FLUXES, NO)
    lnd_flux = land_flux.transpose(1, 0, 2).reshape(FLUXES, NL)
    return (atm_flux, ocn_flux, lnd_flux)
```

```python
import functools

import jax
import jax.numpy as jnp
from jax import lax
from jax.experimental import pallas as pl
from jax.experimental.pallas import tpu as pltpu
from jax.sharding import PartitionSpec as P

ocean_coef = (1.2, 0.9, 1.5, 0.7, 1.1, 1.3, 0.8, 1.0)
ice_coef = (0.5, 1.4, 0.6, 1.2, 0.9, 0.4, 1.6, 0.7)
land_coef = (0.8, 1.1, 0.6, 1.5, 0.7, 1.2, 1.0, 0.5)

GROUP = 8


def coef_column(coef, width):
    row = lax.broadcasted_iota(jnp.int32, (len(coef), width), 0)
    out = jnp.full((len(coef), width), coef[0], jnp.float32)
    for j in range(1, len(coef)):
        out = jnp.where(row == j, coef[j], out)
    return out


def coupler_kernel(
    sizes,
    pick,
    target,
    atm,
    ocn_state,
    ice_state,
    ice_level,
    lnd_state,
    lnd_level,
    ocn_tiles,
    lnd_tiles,
    atm_out,
    ocn_out,
    lnd_out,
    own,
    held,
    tiles,
    so,
    si,
    li,
    sl,
    ll,
    mix,
    terms,
    ocn_v,
    lnd_v,
    outbox,
    inbox,
    own_sum,
    final,
    own_sem,
    keep_sem,
    state_sem,
    tile_sem,
    out_sem,
    send_sem,
    recv_sem,
    back_send,
    back_recv,
):
    sects, cells, ocean_blocks, land_blocks, blocks_here, block, pieces = sizes
    count = sects * cells
    half = cells // 2
    blocks = ocean_blocks + land_blocks
    me = lax.axis_index("sect") * cells + lax.axis_index("cell")
    parity = lax.rem(me, 2)
    delta = 1 - 2 * parity

    def device(number):
        number = lax.rem(number + 2 * count, count)
        return {"sect": lax.div(number, cells), "cell": lax.rem(number, cells)}

    own_copies = []
    for b in range(blocks_here):
        src = atm.at[:, b * block : (b + 1) * block]
        copy = pltpu.make_async_copy(src, own.at[b], own_sem.at[b])
        copy.start()
        own_copies.append(copy)
    tile_copies = []
    for g in range(blocks // GROUP):
        first = g * GROUP
        if first < ocean_blocks:
            src = ocn_tiles.at[pl.ds(first, GROUP)]
        else:
            src = lnd_tiles.at[pl.ds(first - ocean_blocks, GROUP)]
        copy = pltpu.make_async_copy(src, tiles.at[pl.ds(first, GROUP)], tile_sem.at[g])
        copy.start()
        tile_copies.append(copy)
    state_copies = [
        pltpu.make_async_copy(src, dst, state_sem.at[i])
        for i, (src, dst) in enumerate(
            ((ocn_state, so), (ice_state, si), (ice_level, li), (lnd_state, sl), (lnd_level, ll))
        )
    ]
    for copy in state_copies:
        copy.start()

    barrier = pltpu.get_barrier_semaphore()
    greet = [d for d in range(-half, half + 1) if d != 0] + [cells - 1, 1 - cells]
    for d in greet:
        pl.semaphore_signal(
            barrier, inc=1, device_id=device(me + d), device_id_type=pl.DeviceIdType.MESH
        )
    pl.semaphore_wait(barrier, len(greet))
    for copy in own_copies:
        copy.wait()
    keep_copy = pltpu.make_async_copy(own, held.at[pl.ds(half * blocks_here, blocks_here)], keep_sem)
    keep_copy.start()

    width = blocks_here // pieces
    evens = sorted((d for d in range(1 - half, half + 1) if d % 2 == 0 and d != 0), key=lambda d: abs(d))

    def push(slot_here, slot_there, peer, piece, sem):
        here = pl.ds(slot_here * blocks_here + piece * width, width)
        there = pl.ds(slot_there * blocks_here + piece * width, width)
        src = own.at[pl.ds(piece * width, width)] if slot_here == half else held.at[here]
        return pltpu.make_async_remote_copy(
            src_ref=src,
            dst_ref=held.at[there],
            send_sem=send_sem.at[sem, piece],
            recv_sem=recv_sem.at[slot_there, piece],
            device_id=device(peer),
            device_id_type=pl.DeviceIdType.MESH,
        )

    def relay(d, piece, sem):
        moved = d + delta
        wrap = jnp.where(moved == half + 1, cells, 0)
        slot = half - moved + wrap
        return push(half - d, slot, me + delta - wrap, piece, sem)

    sends = []
    for piece in range(pieces):
        for i, d in enumerate(evens):
            sends.append(push(half, half - d, me + d, piece, i))
            sends[-1].start()
        sends.append(relay(0, piece, len(evens)))
        sends[-1].start()

    def source(d, k):
        return held[pick[4 * d + k]]

    def product(d, k):
        lhs = jnp.concatenate([source(d, k), source(d, k + 1)], axis=1)
        rhs = tiles[d, k : k + 2].reshape(2 * block, block)
        return jnp.dot(lhs, rhs, preferred_element_type=jnp.float32)

    def local_source(d, k):
        return own[pick[4 * d + k]]

    def local_group(g):
        for u in range(GROUP):
            d = g * GROUP + u
            lhs = jnp.concatenate([local_source(d, 2), local_source(d, 3)], axis=1)
            rhs = tiles[d, 2:4].reshape(2 * block, block)
            row = pl.multiple_of(d * 24, 24)
            mix[pl.ds(row, 24), :] = jnp.dot(lhs, rhs, preferred_element_type=jnp.float32)

    relays = [(piece, i, d) for piece in range(pieces) for i, d in enumerate(evens)]

    def do_relay(piece, i, d):
        push(half, half - d, me + 1, piece, i).wait_recv()
        sends.append(relay(d, piece, len(evens) + 1 + i))
        sends[-1].start()

    groups = blocks // GROUP
    for g in range(groups):
        tile_copies[g].wait()

    @pl.loop(0, groups)
    def _(g):
        local_group(g)

    for piece, i, d in relays:
        do_relay(piece, i, d)
    for copy in state_copies:
        copy.wait()
    keep_copy.wait()
    for piece in range(pieces):
        for d in range(1 - half, half + 1):
            if d % 2 != 0:
                push(half, half - d, me + 1, piece, 0).wait_recv()

    ocean_c = coef_column(ocean_coef, block)
    ice_c = coef_column(ice_coef, block)
    land_c = coef_column(land_coef, block)

    def winds(d):
        row = d * 24
        u = mix[pl.ds(row, 8, 3), :]
        v = mix[pl.ds(row + 1, 8, 3), :]
        s = mix[pl.ds(row + 2, 8, 3), :]
        return jnp.sqrt(1.0 + u * u + v * v), s

    def back(d, flux):
        out = lax.dot_general(
            flux.astype(jnp.bfloat16),
            tiles[d].reshape(4 * block, block),
            (((1,), (1,)), ((), ())),
            preferred_element_type=jnp.float32,
        )
        for k in range(4):
            row = pl.multiple_of((4 * d + k) * 8, 8)
            terms[pl.ds(row, 8), :] = out[:, k * block : (k + 1) * block]

    def forward_group(first):
        for u in range(GROUP):
            d = first + u
            row = pl.multiple_of(d * 24, 24)
            mix[pl.ds(row, 24), :] = mix[pl.ds(row, 24), :] + product(d, 0)

    @pl.loop(0, ocean_blocks // GROUP)
    def _(g):
        forward_group(g * GROUP)
        for u in range(GROUP):
            d = g * GROUP + u
            lanes = pl.ds(pl.multiple_of(d * block, block), block)
            wind, scalar = winds(d)
            ice = li[pl.ds(d, 1), :].astype(jnp.float32) / 8.0
            flux = (1.0 - ice) * (ocean_c * wind * (scalar - so[:, lanes])) + ice * (
                ice_c * wind * (scalar - si[:, lanes])
            )
            ocn_v[:, lanes] = flux
            back(d, flux)

    @pl.loop(0, land_blocks // GROUP)
    def _(g):
        forward_group(ocean_blocks + g * GROUP)
        for u in range(GROUP):
            e = g * GROUP + u
            d = ocean_blocks + e
            lanes = pl.ds(pl.multiple_of(e * block, block), block)
            wind, scalar = winds(d)
            part = ll[pl.ds(e, 1), :].astype(jnp.float32) / 8.0
            flux = part * (land_c * wind * (scalar - sl[:, lanes]))
            lnd_v[:, lanes] = flux
            back(d, flux)

    ocn_copy = pltpu.make_async_copy(ocn_v, ocn_out, out_sem.at[0])
    lnd_copy = pltpu.make_async_copy(lnd_v, lnd_out, out_sem.at[1])
    ocn_copy.start()
    lnd_copy.start()

    rows = cells * blocks_here
    chosen = (
        lax.broadcasted_iota(jnp.int32, (rows, 4 * blocks), 0) == target[0:1, :]
    ).astype(jnp.float32).astype(jnp.bfloat16)
    for f in range(0, 8, 2):
        x = jnp.concatenate(
            [terms[pl.ds(f, 4 * blocks, 8), :], terms[pl.ds(f + 1, 4 * blocks, 8), :]], axis=1
        )
        high = x.astype(jnp.bfloat16)
        low = (x - high.astype(jnp.float32)).astype(jnp.bfloat16)
        total = jnp.dot(chosen, high, preferred_element_type=jnp.float32) + jnp.dot(
            chosen, low, preferred_element_type=jnp.float32
        )
        for w in range(cells):
            part = total[w * blocks_here : (w + 1) * blocks_here]
            for j in range(2):
                one = part[:, j * block : (j + 1) * block]
                if w == half:
                    own_sum[f + j] = one
                else:
                    outbox[w, f + j] = one.astype(jnp.bfloat16)

    def ship(w):
        return pltpu.make_async_remote_copy(
            src_ref=outbox.at[w],
            dst_ref=inbox.at[w],
            send_sem=back_send.at[w],
            recv_sem=back_recv.at[w],
            device_id=device(me + w - half),
            device_id_type=pl.DeviceIdType.MESH,
        )

    others = sorted((w for w in range(cells) if w != half), key=lambda w: -abs(w - half))
    shipped = [ship(w) for w in others]
    for copy in shipped:
        copy.start()
    for copy in shipped:
        copy.wait_recv()
    for f in range(8):
        value = own_sum[f]
        for w in others:
            value = value + inbox[w, f].astype(jnp.float32)
        final[pl.ds(f, blocks_here, 8), :] = value
    for b in range(blocks_here):
        atm_out[:, b * block : (b + 1) * block] = final[8 * b : 8 * b + 8, :]
    for copy in sends:
        copy.wait_send()
    for copy in shipped:
        copy.wait_send()
    ocn_copy.wait()
    lnd_copy.wait()


def per_device(
    sects,
    cells,
    atm_fields,
    ocn_state,
    ice_state,
    ice_level,
    lnd_state,
    lnd_level,
    ocn_map,
    ocn_local,
    ocn_tiles,
    lnd_map,
    lnd_local,
    lnd_tiles,
):
    fields, width = atm_fields.shape
    block = ocn_tiles.shape[2]
    fluxes = ocn_state.shape[0]
    blocks_here = width // block
    ocean_blocks, land_blocks = ocn_map.shape[0], lnd_map.shape[0]
    blocks = ocean_blocks + land_blocks
    count = sects * cells
    half = cells // 2
    me = lax.axis_index("sect") * cells + lax.axis_index("cell")
    mapped = jnp.concatenate([ocn_map, lnd_map], axis=0)
    local = jnp.concatenate([ocn_local, lnd_local], axis=0)
    span = count * blocks_here
    shifted = lax.rem(mapped + (span - (me - half) * blocks_here), span)
    picks = jnp.concatenate([shifted, local], axis=1).reshape(-1)
    targets = jnp.concatenate([shifted, local + half * blocks_here], axis=1).reshape(1, -1)
    pieces = 2
    evens = half
    any_spec = pl.BlockSpec(memory_space=pl.ANY)
    vmem_spec = pl.BlockSpec(memory_space=pltpu.VMEM)
    sizes = (sects, cells, ocean_blocks, land_blocks, blocks_here, block, pieces)
    f32, bf16 = jnp.float32, jnp.bfloat16
    sem = pltpu.SemaphoreType.DMA
    return pl.pallas_call(
        functools.partial(coupler_kernel, sizes),
        out_shape=(
            jax.ShapeDtypeStruct((fluxes, width), f32),
            jax.ShapeDtypeStruct(ocn_state.shape, f32),
            jax.ShapeDtypeStruct(lnd_state.shape, f32),
        ),
        in_specs=[pl.BlockSpec(memory_space=pltpu.SMEM), vmem_spec] + [any_spec] * 8,
        out_specs=(vmem_spec, any_spec, any_spec),
        scratch_shapes=[
            pltpu.VMEM((blocks_here, fields, block), bf16),
            pltpu.VMEM((cells * blocks_here, fields, block), bf16),
            pltpu.VMEM((blocks, 4, block, block), bf16),
            pltpu.VMEM(ocn_state.shape, f32),
            pltpu.VMEM(ice_state.shape, f32),
            pltpu.VMEM((ocean_blocks, block), jnp.int32),
            pltpu.VMEM(lnd_state.shape, f32),
            pltpu.VMEM((land_blocks, block), jnp.int32),
            pltpu.VMEM((blocks * fields, block), f32),
            pltpu.VMEM((blocks * 4 * fluxes, block), f32),
            pltpu.VMEM(ocn_state.shape, f32),
            pltpu.VMEM(lnd_state.shape, f32),
            pltpu.VMEM((cells, fluxes, blocks_here, block), bf16),
            pltpu.VMEM((cells, fluxes, blocks_here, block), bf16),
            pltpu.VMEM((fluxes, blocks_here, block), f32),
            pltpu.VMEM((blocks_here * fluxes, block), f32),
            sem((blocks_here,)),
            sem,
            sem((5,)),
            sem((blocks // GROUP,)),
            sem((2,)),
            sem((2 * evens, pieces)),
            sem((cells, pieces)),
            sem((cells,)),
            sem((cells,)),
        ],
        compiler_params=pltpu.CompilerParams(collective_id=0, has_side_effects=True),
    )(
        picks,
        targets,
        atm_fields,
        ocn_state,
        ice_state,
        ice_level.reshape(ocean_blocks, block),
        lnd_state,
        lnd_level.reshape(land_blocks, block),
        ocn_tiles,
        lnd_tiles,
    )


def solution(mesh):
    sects, cells = mesh.shape["sect"], mesh.shape["cell"]
    cut = ("sect", "cell")
    wide, flat = P(None, cut), P(cut)
    pair, quad = P(cut, None), P(cut, None, None, None)
    in_specs = (
        wide, wide, wide, flat, wide, flat, pair, pair, quad, pair, pair, quad,
    )
    return jax.shard_map(
        functools.partial(per_device, sects, cells),
        mesh=mesh,
        in_specs=in_specs,
        out_specs=(wide, wide, wide),
        check_vma=False,
    )
```

```python
import functools

import jax
import jax.numpy as jnp
from jax import lax
from jax.experimental import pallas as pl
from jax.experimental.pallas import tpu as pltpu
from jax.sharding import PartitionSpec as P

ocean_coef = (1.2, 0.9, 1.5, 0.7, 1.1, 1.3, 0.8, 1.0)
ice_coef = (0.5, 1.4, 0.6, 1.2, 0.9, 0.4, 1.6, 0.7)
land_coef = (0.8, 1.1, 0.6, 1.5, 0.7, 1.2, 1.0, 0.5)

GROUP = 8


def coef_column(coef, width):
    row = lax.broadcasted_iota(jnp.int32, (len(coef), width), 0)
    out = jnp.full((len(coef), width), coef[0], jnp.float32)
    for j in range(1, len(coef)):
        out = jnp.where(row == j, coef[j], out)
    return out


def coupler_kernel(
    sizes,
    ocn_map,
    ocn_local,
    lnd_map,
    lnd_local,
    atm,
    ocn_state,
    ice_state,
    ice_level,
    lnd_state,
    lnd_level,
    ocn_tiles,
    lnd_tiles,
    atm_out,
    ocn_out,
    lnd_out,
    pick_om,
    pick_ol,
    pick_lm,
    pick_ll,
    col_om,
    col_ol,
    col_lm,
    col_ll,
    own,
    held,
    tiles,
    so,
    si,
    li,
    sl,
    ll,
    mix,
    terms,
    ocn_v,
    lnd_v,
    sums,
    outbox,
    merge_in,
    merged,
    inbox,
    final,
    own_sem,
    keep_sem,
    state_sem,
    tile_sem,
    out_sem,
    send_sem,
    recv_sem,
    merge_send,
    merge_recv,
    back_send,
    back_recv,
):
    sects, cells, ocean_blocks, land_blocks, blocks_here, block, pieces = sizes
    count = sects * cells
    half = cells // 2
    rows = cells // 2
    blocks = ocean_blocks + land_blocks
    my_cell = lax.axis_index("cell")
    me = lax.axis_index("sect") * cells + my_cell
    my_row = lax.div(my_cell, 2)
    side = lax.rem(my_cell, 2)
    across = my_cell + 1 - 2 * side

    def device(number):
        number = lax.rem(number + 2 * count, count)
        return {"sect": lax.div(number, cells), "cell": lax.rem(number, cells)}

    def owner(j):
        return me - half + lax.rem(j - me + half + count, cells)

    def receiver(q, j):
        return q - half + 1 + lax.rem(j - q + half - 1 + 2 * count, cells)

    own_copies = []
    for b in range(blocks_here):
        src = atm.at[:, b * block : (b + 1) * block]
        copy = pltpu.make_async_copy(src, own.at[b], own_sem.at[b])
        copy.start()
        own_copies.append(copy)

    barrier = pltpu.get_barrier_semaphore()
    apart = sorted({1, 2, cells - 1, cells - 2} | set(range(2, half + 1, 2)))
    for d in apart:
        for number in (me + d, me - d):
            pl.semaphore_signal(
                barrier, inc=1, device_id=device(number), device_id_type=pl.DeviceIdType.MESH
            )

    small_copies = [
        pltpu.make_async_copy(src, dst, state_sem.at[i])
        for i, (src, dst) in enumerate(
            (
                (ocn_map, pick_om),
                (ocn_local, pick_ol),
                (lnd_map, pick_lm),
                (lnd_local, pick_ll),
                (ocn_map, col_om),
                (ocn_local, col_ol),
                (lnd_map, col_lm),
                (lnd_local, col_ll),
                (ocn_state, so),
                (ice_state, si),
                (ice_level, li),
                (lnd_state, sl),
                (lnd_level, ll),
            )
        )
    ]
    for copy in small_copies:
        copy.start()
    tile_copies = []
    for g in range(blocks // GROUP):
        first = g * GROUP
        if first < ocean_blocks:
            src = ocn_tiles.at[pl.ds(first, GROUP)]
        else:
            src = lnd_tiles.at[pl.ds(first - ocean_blocks, GROUP)]
        copy = pltpu.make_async_copy(src, tiles.at[pl.ds(first, GROUP)], tile_sem.at[g])
        copy.start()
        tile_copies.append(copy)

    for copy in own_copies:
        copy.wait()
    keep_copy = pltpu.make_async_copy(
        own, held.at[pl.ds(my_cell * blocks_here, blocks_here)], keep_sem
    )
    keep_copy.start()
    pl.semaphore_wait(barrier, 2 * len(apart))

    width = blocks_here // pieces

    def push(j, to_cell, piece, kind, mine):
        here = pl.ds(j * blocks_here + piece * width, width)
        src = own.at[pl.ds(piece * width, width)] if mine else held.at[here]
        return pltpu.make_async_remote_copy(
            src_ref=src,
            dst_ref=held.at[here],
            send_sem=send_sem.at[kind, lax.div(j, 2), piece],
            recv_sem=recv_sem.at[j, piece],
            device_id=device(receiver(owner(j), to_cell)),
            device_id_type=pl.DeviceIdType.MESH,
        )

    def send_up(j, piece, mine):
        return push(j, my_cell + 2, piece, 0, mine)

    def send_down(j, piece, mine):
        return push(j, my_cell - 2, piece, 1, mine)

    def send_across(j, piece, mine):
        return push(j, across, piece, 2, mine)

    for piece in range(pieces):

        @pl.when(my_row < rows - 1)
        def _():
            send_up(my_cell, piece, True).start()

        @pl.when(my_row > 0)
        def _():
            send_down(my_cell, piece, True).start()

        send_across(my_cell, piece, True).start()

    def dot_pair(source, d, refs, e, k):
        lhs = jnp.concatenate([source(refs[e, 0]), source(refs[e, 1])], axis=1)
        rhs = tiles[d, k : k + 2].reshape(2 * block, block)
        return jnp.dot(lhs, rhs, preferred_element_type=jnp.float32)

    span = cells * blocks_here

    def from_held(index):
        return held[lax.rem(index, span)]

    def from_own(index):
        return own[index]

    def local_part(refs, base, first):
        for u in range(GROUP):
            e = first + u
            d = base + e
            row = pl.multiple_of(d * 24, 24)
            mix[pl.ds(row, 24), :] = dot_pair(from_own, d, refs, e, 2)

    def step(k, piece):
        @pl.when(my_row - k >= 0)
        def _():
            j = my_cell - 2 * k
            send_across(j, piece, False).wait_recv()

            @pl.when(my_row < rows - 1)
            def _():
                send_up(j, piece, False).start()

            send_across(j, piece, False).start()

        @pl.when(my_row + k < rows)
        def _():
            j = my_cell + 2 * k
            send_across(j, piece, False).wait_recv()

            @pl.when(my_row > 0)
            def _():
                send_down(j, piece, False).start()

            send_across(j, piece, False).start()

    for copy in small_copies:
        copy.wait()
    for copy in tile_copies:
        copy.wait()

    @pl.loop(0, ocean_blocks // GROUP // 2)
    def _(g):
        local_part(pick_ol, 0, g * GROUP)

    step(1, 0)

    @pl.loop(ocean_blocks // GROUP // 2, ocean_blocks // GROUP)
    def _(g):
        local_part(pick_ol, 0, g * GROUP)

    @pl.loop(0, land_blocks // GROUP)
    def _(g):
        local_part(pick_ll, ocean_blocks, g * GROUP)

    for k in range(1, rows):
        for piece in range(pieces):
            if (k, piece) != (1, 0):
                step(k, piece)
    keep_copy.wait()

    lanes_of = lax.broadcasted_iota(jnp.int32, (1, span), 1)
    columns = []
    for k in range(4):
        if k < 2:
            pair = (lax.rem(col_om[...], span), lax.rem(col_lm[...], span))
        else:
            pair = (
                col_ol[...] + my_cell * blocks_here,
                col_ll[...] + my_cell * blocks_here,
            )
        columns += [part[:, k % 2 : k % 2 + 1] for part in pair]
    marks = jnp.concatenate(
        [(column == lanes_of).astype(jnp.float32) for column in columns], axis=0
    )
    chosen = marks.T.astype(jnp.bfloat16)

    for r in range(rows):
        for piece in range(pieces):
            send_across(2 * r + 1 - side, piece, False).wait_recv()

    ocean_c = coef_column(ocean_coef, block)
    ice_c = coef_column(ice_coef, block)
    land_c = coef_column(land_coef, block)

    def winds(d):
        row = d * 24
        u = mix[pl.ds(row, 8, 3), :]
        v = mix[pl.ds(row + 1, 8, 3), :]
        s = mix[pl.ds(row + 2, 8, 3), :]
        return jnp.sqrt(1.0 + u * u + v * v), s

    def back(d, flux):
        out = lax.dot_general(
            flux.astype(jnp.bfloat16),
            tiles[d].reshape(4 * block, block),
            (((1,), (1,)), ((), ())),
            preferred_element_type=jnp.float32,
        )
        for k in range(4):
            row = pl.multiple_of((k * blocks + d) * 8, 8)
            terms[pl.ds(row, 8), :] = out[:, k * block : (k + 1) * block]

    def forward_part(refs, base, first):
        for u in range(GROUP):
            e = first + u
            d = base + e
            row = pl.multiple_of(d * 24, 24)
            mix[pl.ds(row, 24), :] = mix[pl.ds(row, 24), :] + dot_pair(from_held, d, refs, e, 0)

    @pl.loop(0, ocean_blocks // GROUP)
    def _(g):
        forward_part(pick_om, 0, g * GROUP)
        for u in range(GROUP):
            d = g * GROUP + u
            lanes = pl.ds(pl.multiple_of(d * block, block), block)
            wind, scalar = winds(d)
            ice = li[pl.ds(d, 1), :].astype(jnp.float32) / 8.0
            flux = (1.0 - ice) * (ocean_c * wind * (scalar - so[:, lanes])) + ice * (
                ice_c * wind * (scalar - si[:, lanes])
            )
            ocn_v[:, lanes] = flux
            back(d, flux)

    @pl.loop(0, land_blocks // GROUP)
    def _(g):
        forward_part(pick_lm, ocean_blocks, g * GROUP)
        for u in range(GROUP):
            e = g * GROUP + u
            d = ocean_blocks + e
            lanes = pl.ds(pl.multiple_of(e * block, block), block)
            wind, scalar = winds(d)
            part = ll[pl.ds(e, 1), :].astype(jnp.float32) / 8.0
            flux = part * (land_c * wind * (scalar - sl[:, lanes]))
            lnd_v[:, lanes] = flux
            back(d, flux)

    ocn_copy = pltpu.make_async_copy(ocn_v, ocn_out, out_sem.at[0])
    lnd_copy = pltpu.make_async_copy(lnd_v, lnd_out, out_sem.at[1])
    ocn_copy.start()
    lnd_copy.start()

    for f in range(0, 8, 2):
        x = jnp.concatenate(
            [terms[pl.ds(f, 4 * blocks, 8), :], terms[pl.ds(f + 1, 4 * blocks, 8), :]], axis=1
        )
        high = x.astype(jnp.bfloat16)
        low = (x - high.astype(jnp.float32)).astype(jnp.bfloat16)
        total = jnp.dot(chosen, high, preferred_element_type=jnp.float32) + jnp.dot(
            chosen, low, preferred_element_type=jnp.float32
        )
        sums[f] = total[:, :block]
        sums[f + 1] = total[:, block:]

    def part_of(f, j):
        return sums[f, pl.ds(pl.multiple_of(j * blocks_here, blocks_here), blocks_here), :]

    def merge(r):
        j = 2 * r + 1 - side
        return pltpu.make_async_remote_copy(
            src_ref=outbox.at[r],
            dst_ref=merge_in.at[r],
            send_sem=merge_send.at[r],
            recv_sem=merge_recv.at[r],
            device_id=device(receiver(owner(j), across)),
            device_id_type=pl.DeviceIdType.MESH,
        )

    def ship(r):
        return pltpu.make_async_remote_copy(
            src_ref=merged.at[r],
            dst_ref=inbox.at[my_row],
            send_sem=back_send.at[r],
            recv_sem=back_recv.at[my_row],
            device_id=device(owner(2 * r + side)),
            device_id_type=pl.DeviceIdType.MESH,
        )

    def arrival(r):
        return pltpu.make_async_remote_copy(
            src_ref=merged.at[r],
            dst_ref=inbox.at[r],
            send_sem=back_send.at[r],
            recv_sem=back_recv.at[r],
            device_id=device(me + 1),
            device_id_type=pl.DeviceIdType.MESH,
        )

    order = [lax.rem(my_row + k, rows) for k in list(range(1, rows)) + [0]]
    for r in order:
        for f in range(8):
            outbox[r, f] = part_of(f, 2 * r + 1 - side).astype(jnp.bfloat16)
        merge(r).start()
    for r in order[:-1]:
        merge(r).wait_recv()
        for f in range(8):
            merged[r, f] = (
                part_of(f, 2 * r + side) + merge_in[r, f].astype(jnp.float32)
            ).astype(jnp.bfloat16)
        ship(r).start()
    merge(my_row).wait_recv()
    for r in order[:-1]:
        arrival(r).wait_recv()
    for f in range(8):
        value = part_of(f, my_cell) + merge_in[my_row, f].astype(jnp.float32)
        for r in order[:-1]:
            value = value + inbox[r, f].astype(jnp.float32)
        final[pl.ds(f, blocks_here, 8), :] = value
    for b in range(blocks_here):
        atm_out[:, b * block : (b + 1) * block] = final[8 * b : 8 * b + 8, :]
    for r in range(rows):
        j = 2 * r + side
        for piece in range(pieces):
            send_across(j, piece, False).wait_send()

            @pl.when((r <= my_row) & (my_row < rows - 1))
            def _():
                send_up(j, piece, False).wait_send()

            @pl.when((r >= my_row) & (my_row > 0))
            def _():
                send_down(j, piece, False).wait_send()

        merge(r).wait_send()
    for r in order[:-1]:
        ship(r).wait_send()
    ocn_copy.wait()
    lnd_copy.wait()


def finish_kernel(a, b, c, a_out, b_out, c_out):
    a_out[...] = a[...]
    b_out[...] = b[...]
    c_out[...] = c[...]


def per_device(
    sects,
    cells,
    atm_fields,
    ocn_state,
    ice_state,
    ice_level,
    lnd_state,
    lnd_level,
    ocn_map,
    ocn_local,
    ocn_tiles,
    lnd_map,
    lnd_local,
    lnd_tiles,
):
    fields, width = atm_fields.shape
    block = ocn_tiles.shape[2]
    fluxes = ocn_state.shape[0]
    blocks_here = width // block
    ocean_blocks, land_blocks = ocn_map.shape[0], lnd_map.shape[0]
    blocks = ocean_blocks + land_blocks
    pieces = 2
    rows = cells // 2
    any_spec = pl.BlockSpec(memory_space=pl.ANY)
    vmem_spec = pl.BlockSpec(memory_space=pltpu.VMEM)
    sizes = (sects, cells, ocean_blocks, land_blocks, blocks_here, block, pieces)
    f32, bf16, i32 = jnp.float32, jnp.bfloat16, jnp.int32
    sem = pltpu.SemaphoreType.DMA
    shapes = (
        jax.ShapeDtypeStruct((fluxes, width), f32),
        jax.ShapeDtypeStruct(ocn_state.shape, f32),
        jax.ShapeDtypeStruct(lnd_state.shape, f32),
    )
    maps = (ocn_map.shape, ocn_local.shape, lnd_map.shape, lnd_local.shape)
    results = pl.pallas_call(
        functools.partial(coupler_kernel, sizes),
        out_shape=shapes,
        in_specs=[any_spec] * 12,
        out_specs=(vmem_spec, any_spec, any_spec),
        scratch_shapes=[pltpu.SMEM(shape, i32) for shape in maps]
        + [pltpu.VMEM(shape, i32) for shape in maps]
        + [
            pltpu.VMEM((blocks_here, fields, block), bf16),
            pltpu.VMEM((cells * blocks_here, fields, block), bf16),
            pltpu.VMEM((blocks, 4, block, block), bf16),
            pltpu.VMEM(ocn_state.shape, f32),
            pltpu.VMEM(ice_state.shape, f32),
            pltpu.VMEM((ocean_blocks, block), i32),
            pltpu.VMEM(lnd_state.shape, f32),
            pltpu.VMEM((land_blocks, block), i32),
            pltpu.VMEM((blocks * fields, block), f32),
            pltpu.VMEM((blocks * 4 * fluxes, block), f32),
            pltpu.VMEM(ocn_state.shape, f32),
            pltpu.VMEM(lnd_state.shape, f32),
            pltpu.VMEM((fluxes, cells * blocks_here, block), f32),
            pltpu.VMEM((rows, fluxes, blocks_here, block), bf16),
            pltpu.VMEM((rows, fluxes, blocks_here, block), bf16),
            pltpu.VMEM((rows, fluxes, blocks_here, block), bf16),
            pltpu.VMEM((rows, fluxes, blocks_here, block), bf16),
            pltpu.VMEM((blocks_here * fluxes, block), f32),
            sem((blocks_here,)),
            sem,
            sem((13,)),
            sem((blocks // GROUP,)),
            sem((2,)),
            sem((3, rows, pieces)),
            sem((cells, pieces)),
            sem((rows,)),
            sem((rows,)),
            sem((rows,)),
            sem((rows,)),
        ],
        compiler_params=pltpu.CompilerParams(collective_id=0, has_side_effects=True),
    )(
        ocn_map,
        ocn_local,
        lnd_map,
        lnd_local,
        atm_fields,
        ocn_state,
        ice_state,
        ice_level.reshape(ocean_blocks, block),
        lnd_state,
        lnd_level.reshape(land_blocks, block),
        ocn_tiles,
        lnd_tiles,
    )
    return pl.pallas_call(
        finish_kernel,
        out_shape=shapes,
        in_specs=[vmem_spec] * 3,
        out_specs=(vmem_spec,) * 3,
    )(*results)


def solution(mesh):
    sects, cells = mesh.shape["sect"], mesh.shape["cell"]
    cut = ("sect", "cell")
    wide, flat = P(None, cut), P(cut)
    pair, quad = P(cut, None), P(cut, None, None, None)
    in_specs = (
        wide, wide, wide, flat, wide, flat, pair, pair, quad, pair, pair, quad,
    )
    return jax.shard_map(
        functools.partial(per_device, sects, cells),
        mesh=mesh,
        in_specs=in_specs,
        out_specs=(wide, wide, wide),
        check_vma=False,
    )
```

```python
import functools

import jax
import jax.numpy as jnp
from jax import lax
from jax.experimental import pallas as pl
from jax.experimental.pallas import tpu as pltpu
from jax.sharding import PartitionSpec as P

ocean_coef = (1.2, 0.9, 1.5, 0.7, 1.1, 1.3, 0.8, 1.0)
ice_coef = (0.5, 1.4, 0.6, 1.2, 0.9, 0.4, 1.6, 0.7)
land_coef = (0.8, 1.1, 0.6, 1.5, 0.7, 1.2, 1.0, 0.5)

GROUP = 8
DEPTH = 4


def coef_column(coef, width):
    row = lax.broadcasted_iota(jnp.int32, (len(coef), width), 0)
    out = jnp.full((len(coef), width), coef[0], jnp.float32)
    for j in range(1, len(coef)):
        out = jnp.where(row == j, coef[j], out)
    return out


def coupler_kernel(
    sizes,
    ocn_map,
    ocn_local,
    lnd_map,
    lnd_local,
    atm,
    ocn_state,
    ice_state,
    ice_level,
    lnd_state,
    lnd_level,
    ocn_tiles,
    lnd_tiles,
    atm_out,
    ocn_out,
    lnd_out,
    pick_om,
    pick_ol,
    pick_lm,
    pick_ll,
    col_om,
    col_ol,
    col_lm,
    col_ll,
    own,
    held,
    tiles,
    so,
    si,
    li,
    sl,
    ll,
    mix,
    terms,
    ocn_v,
    lnd_v,
    sums,
    outbox,
    merge_in,
    merged,
    inbox,
    final,
    own_sem,
    keep_sem,
    state_sem,
    tile_sem,
    out_sem,
    send_sem,
    recv_sem,
    merge_send,
    merge_recv,
    back_send,
    back_recv,
):
    sects, cells, ocean_blocks, land_blocks, blocks_here, block, pieces = sizes
    count = sects * cells
    half = cells // 2
    rows = cells // 2
    blocks = ocean_blocks + land_blocks
    my_cell = lax.axis_index("cell")
    me = lax.axis_index("sect") * cells + my_cell
    my_row = lax.div(my_cell, 2)
    side = lax.rem(my_cell, 2)
    across = my_cell + 1 - 2 * side

    def device(number):
        number = lax.rem(number + 2 * count, count)
        return {"sect": lax.div(number, cells), "cell": lax.rem(number, cells)}

    def owner(j):
        return me - half + lax.rem(j - me + half + count, cells)

    def receiver(q, j):
        return q - half + 1 + lax.rem(j - q + half - 1 + 2 * count, cells)

    own_copies = []
    for b in range(blocks_here):
        src = atm.at[:, b * block : (b + 1) * block]
        copy = pltpu.make_async_copy(src, own.at[b], own_sem.at[b])
        copy.start()
        own_copies.append(copy)

    barrier = pltpu.get_barrier_semaphore()
    apart = sorted({1, 2, cells - 1, cells - 2} | set(range(2, half + 1, 2)))
    for d in apart:
        for number in (me + d, me - d):
            pl.semaphore_signal(
                barrier, inc=1, device_id=device(number), device_id_type=pl.DeviceIdType.MESH
            )

    small_copies = [
        pltpu.make_async_copy(src, dst, state_sem.at[i])
        for i, (src, dst) in enumerate(
            (
                (ocn_map, pick_om),
                (ocn_local, pick_ol),
                (lnd_map, pick_lm),
                (lnd_local, pick_ll),
                (ocn_map, col_om),
                (ocn_local, col_ol),
                (lnd_map, col_lm),
                (lnd_local, col_ll),
                (ocn_state, so),
                (ice_state, si),
                (ice_level, li),
                (lnd_state, sl),
                (lnd_level, ll),
            )
        )
    ]
    for copy in small_copies:
        copy.start()
    tile_copies = []
    for g in range(blocks // GROUP):
        first = g * GROUP
        if first < ocean_blocks:
            src = ocn_tiles.at[pl.ds(first, GROUP)]
        else:
            src = lnd_tiles.at[pl.ds(first - ocean_blocks, GROUP)]
        copy = pltpu.make_async_copy(src, tiles.at[pl.ds(first, GROUP)], tile_sem.at[g])
        copy.start()
        tile_copies.append(copy)

    for copy in own_copies:
        copy.wait()
    keep_copy = pltpu.make_async_copy(
        own, held.at[pl.ds(my_cell * blocks_here, blocks_here)], keep_sem
    )
    keep_copy.start()
    pl.semaphore_wait(barrier, 2 * len(apart))

    width = blocks_here // pieces

    def push(j, to_cell, piece, kind, mine):
        here = pl.ds(j * blocks_here + piece * width, width)
        src = own.at[pl.ds(piece * width, width)] if mine else held.at[here]
        return pltpu.make_async_remote_copy(
            src_ref=src,
            dst_ref=held.at[here],
            send_sem=send_sem.at[kind, lax.div(j, 2), piece],
            recv_sem=recv_sem.at[j, piece],
            device_id=device(receiver(owner(j), to_cell)),
            device_id_type=pl.DeviceIdType.MESH,
        )

    def send_up(j, piece, mine):
        return push(j, my_cell + 2, piece, 0, mine)

    def send_down(j, piece, mine):
        return push(j, my_cell - 2, piece, 1, mine)

    def send_across(j, piece, mine):
        return push(j, across, piece, 2, mine)

    for piece in range(pieces):

        @pl.when(my_row < rows - 1)
        def _():
            send_up(my_cell, piece, True).start()

        @pl.when(my_row > 0)
        def _():
            send_down(my_cell, piece, True).start()

        send_across(my_cell, piece, True).start()

    def dot_pair(source, d, refs, e, k):
        lhs = jnp.concatenate([source(refs[0, e]), source(refs[1, e])], axis=1)
        rhs = tiles[d, k : k + 2].reshape(2 * block, block)
        return jnp.dot(lhs, rhs, preferred_element_type=jnp.float32)

    span = cells * blocks_here

    def from_held(index):
        return held[lax.rem(index, span)]

    def from_own(index):
        return own[index]

    def local_part(refs, base, first):
        for u in range(GROUP):
            e = first + u
            d = base + e
            row = pl.multiple_of(d * 24, 24)
            mix[pl.ds(row, 24), :] = dot_pair(from_own, d, refs, e, 2)

    def step(k, piece):
        @pl.when(my_row - k >= 0)
        def _():
            j = my_cell - 2 * k
            send_across(j, piece, False).wait_recv()

            @pl.when(my_row < rows - 1)
            def _():
                send_up(j, piece, False).start()

            send_across(j, piece, False).start()

        @pl.when(my_row + k < rows)
        def _():
            j = my_cell + 2 * k
            send_across(j, piece, False).wait_recv()

            @pl.when(my_row > 0)
            def _():
                send_down(j, piece, False).start()

            send_across(j, piece, False).start()

    for copy in small_copies:
        copy.wait()
    for copy in tile_copies:
        copy.wait()

    @pl.loop(0, ocean_blocks // GROUP // 2)
    def _(g):
        local_part(pick_ol, 0, g * GROUP)

    step(1, 0)

    @pl.loop(ocean_blocks // GROUP // 2, ocean_blocks // GROUP)
    def _(g):
        local_part(pick_ol, 0, g * GROUP)

    @pl.loop(0, land_blocks // GROUP)
    def _(g):
        local_part(pick_ll, ocean_blocks, g * GROUP)

    for k in range(1, rows):
        for piece in range(pieces):
            if (k, piece) != (1, 0):
                step(k, piece)
    keep_copy.wait()

    parts = []
    for k in range(4):
        for mapped, local in ((col_om, col_ol), (col_lm, col_ll)):
            if k < 2:
                parts.append(lax.rem(mapped[k : k + 1, :], span))
            else:
                parts.append(local[k - 2 : k - 1, :] + my_cell * blocks_here)
    target = jnp.concatenate(parts, axis=1)
    chosen = (
        (lax.broadcasted_iota(jnp.int32, (span, 4 * blocks), 0) == target)
        .astype(jnp.float32)
        .astype(jnp.bfloat16)
    )

    for r in range(rows):
        for piece in range(pieces):
            send_across(2 * r + 1 - side, piece, False).wait_recv()

    ocean_c = coef_column(ocean_coef, block)
    ice_c = coef_column(ice_coef, block)
    land_c = coef_column(land_coef, block)

    def winds(d):
        row = d * 24
        u = mix[pl.ds(row, 8, 3), :]
        v = mix[pl.ds(row + 1, 8, 3), :]
        s = mix[pl.ds(row + 2, 8, 3), :]
        return jnp.sqrt(1.0 + u * u + v * v), s

    def back(d, flux):
        out = lax.dot_general(
            flux.astype(jnp.bfloat16),
            tiles[d].reshape(4 * block, block),
            (((1,), (1,)), ((), ())),
            preferred_element_type=jnp.float32,
        )
        for k in range(4):
            row = pl.multiple_of((k * blocks + d) * 8, 8)
            terms[pl.ds(row, 8), :] = out[:, k * block : (k + 1) * block]

    def forward_part(refs, base, first):
        for u in range(GROUP):
            e = first + u
            d = base + e
            row = pl.multiple_of(d * 24, 24)
            mix[pl.ds(row, 24), :] = mix[pl.ds(row, 24), :] + dot_pair(from_held, d, refs, e, 0)

    @pl.loop(0, ocean_blocks // GROUP)
    def _(g):
        forward_part(pick_om, 0, g * GROUP)
        for u in range(GROUP):
            d = g * GROUP + u
            lanes = pl.ds(pl.multiple_of(d * block, block), block)
            wind, scalar = winds(d)
            ice = li[pl.ds(d, 1), :].astype(jnp.float32) / 8.0
            flux = (1.0 - ice) * (ocean_c * wind * (scalar - so[:, lanes])) + ice * (
                ice_c * wind * (scalar - si[:, lanes])
            )
            ocn_v[:, lanes] = flux
            back(d, flux)

    @pl.loop(0, land_blocks // GROUP)
    def _(g):
        forward_part(pick_lm, ocean_blocks, g * GROUP)
        for u in range(GROUP):
            e = g * GROUP + u
            d = ocean_blocks + e
            lanes = pl.ds(pl.multiple_of(e * block, block), block)
            wind, scalar = winds(d)
            part = ll[pl.ds(e, 1), :].astype(jnp.float32) / 8.0
            flux = part * (land_c * wind * (scalar - sl[:, lanes]))
            lnd_v[:, lanes] = flux
            back(d, flux)

    ocn_copy = pltpu.make_async_copy(ocn_v, ocn_out, out_sem.at[0])
    lnd_copy = pltpu.make_async_copy(lnd_v, lnd_out, out_sem.at[1])
    ocn_copy.start()
    lnd_copy.start()

    for f in range(0, 8, 2):
        x = jnp.concatenate(
            [terms[pl.ds(f, 4 * blocks, 8), :], terms[pl.ds(f + 1, 4 * blocks, 8), :]], axis=1
        )
        high = x.astype(jnp.bfloat16)
        low = (x - high.astype(jnp.float32)).astype(jnp.bfloat16)
        total = jnp.dot(chosen, high, preferred_element_type=jnp.float32) + jnp.dot(
            chosen, low, preferred_element_type=jnp.float32
        )
        sums[f] = total[:, :block]
        sums[f + 1] = total[:, block:]

    def part_of(f, j):
        return sums[f, pl.ds(pl.multiple_of(j * blocks_here, blocks_here), blocks_here), :]

    def merge(r):
        j = 2 * r + 1 - side
        return pltpu.make_async_remote_copy(
            src_ref=outbox.at[r],
            dst_ref=merge_in.at[r],
            send_sem=merge_send.at[r],
            recv_sem=merge_recv.at[r],
            device_id=device(receiver(owner(j), across)),
            device_id_type=pl.DeviceIdType.MESH,
        )

    def ship(r):
        return pltpu.make_async_remote_copy(
            src_ref=merged.at[r],
            dst_ref=inbox.at[my_row],
            send_sem=back_send.at[r],
            recv_sem=back_recv.at[my_row],
            device_id=device(owner(2 * r + side)),
            device_id_type=pl.DeviceIdType.MESH,
        )

    def arrival(r):
        return pltpu.make_async_remote_copy(
            src_ref=merged.at[r],
            dst_ref=inbox.at[r],
            send_sem=back_send.at[r],
            recv_sem=back_recv.at[r],
            device_id=device(me + 1),
            device_id_type=pl.DeviceIdType.MESH,
        )

    order = [lax.rem(my_row + k, rows) for k in list(range(1, rows)) + [0]]
    for i, r in enumerate(order):
        for f in range(8):
            outbox[r, f] = part_of(f, 2 * r + 1 - side).astype(jnp.bfloat16)
        if i >= DEPTH:
            merge(order[i - DEPTH]).wait_send()
        merge(r).start()
    for r in order[:-1]:
        merge(r).wait_recv()
        for f in range(8):
            merged[r, f] = (
                part_of(f, 2 * r + side) + merge_in[r, f].astype(jnp.float32)
            ).astype(jnp.bfloat16)
        ship(r).start()
    merge(my_row).wait_recv()
    for r in order[:-1]:
        arrival(r).wait_recv()
    for f in range(8):
        value = part_of(f, my_cell) + merge_in[my_row, f].astype(jnp.float32)
        for r in order[:-1]:
            value = value + inbox[r, f].astype(jnp.float32)
        final[pl.ds(f, blocks_here, 8), :] = value
    for b in range(blocks_here):
        atm_out[:, b * block : (b + 1) * block] = final[8 * b : 8 * b + 8, :]
    for r in range(rows):
        j = 2 * r + side
        for piece in range(pieces):
            send_across(j, piece, False).wait_send()

            @pl.when((r <= my_row) & (my_row < rows - 1))
            def _():
                send_up(j, piece, False).wait_send()

            @pl.when((r >= my_row) & (my_row > 0))
            def _():
                send_down(j, piece, False).wait_send()

    for r in order[-DEPTH:]:
        merge(r).wait_send()
    for r in order[:-1]:
        ship(r).wait_send()
    ocn_copy.wait()
    lnd_copy.wait()


def finish_kernel(a, b, c, a_out, b_out, c_out):
    a_out[...] = a[...]
    b_out[...] = b[...]
    c_out[...] = c[...]


def per_device(
    sects,
    cells,
    atm_fields,
    ocn_state,
    ice_state,
    ice_level,
    lnd_state,
    lnd_level,
    ocn_map,
    ocn_local,
    ocn_tiles,
    lnd_map,
    lnd_local,
    lnd_tiles,
):
    fields, width = atm_fields.shape
    block = ocn_tiles.shape[2]
    fluxes = ocn_state.shape[0]
    blocks_here = width // block
    ocean_blocks, land_blocks = ocn_map.shape[0], lnd_map.shape[0]
    blocks = ocean_blocks + land_blocks
    pieces = 2
    rows = cells // 2
    any_spec = pl.BlockSpec(memory_space=pl.ANY)
    vmem_spec = pl.BlockSpec(memory_space=pltpu.VMEM)
    sizes = (sects, cells, ocean_blocks, land_blocks, blocks_here, block, pieces)
    f32, bf16, i32 = jnp.float32, jnp.bfloat16, jnp.int32
    sem = pltpu.SemaphoreType.DMA
    shapes = (
        jax.ShapeDtypeStruct((fluxes, width), f32),
        jax.ShapeDtypeStruct(ocn_state.shape, f32),
        jax.ShapeDtypeStruct(lnd_state.shape, f32),
    )
    maps = [x.shape[::-1] for x in (ocn_map, ocn_local, lnd_map, lnd_local)]
    results = pl.pallas_call(
        functools.partial(coupler_kernel, sizes),
        out_shape=shapes,
        in_specs=[any_spec] * 12,
        out_specs=(vmem_spec, any_spec, any_spec),
        scratch_shapes=[pltpu.SMEM(shape, i32) for shape in maps]
        + [pltpu.VMEM(shape, i32) for shape in maps]
        + [
            pltpu.VMEM((blocks_here, fields, block), bf16),
            pltpu.VMEM((cells * blocks_here, fields, block), bf16),
            pltpu.VMEM((blocks, 4, block, block), bf16),
            pltpu.VMEM(ocn_state.shape, f32),
            pltpu.VMEM(ice_state.shape, f32),
            pltpu.VMEM((ocean_blocks, block), i32),
            pltpu.VMEM(lnd_state.shape, f32),
            pltpu.VMEM((land_blocks, block), i32),
            pltpu.VMEM((blocks * fields, block), f32),
            pltpu.VMEM((blocks * 4 * fluxes, block), f32),
            pltpu.VMEM(ocn_state.shape, f32),
            pltpu.VMEM(lnd_state.shape, f32),
            pltpu.VMEM((fluxes, cells * blocks_here, block), f32),
            pltpu.VMEM((rows, fluxes, blocks_here, block), bf16),
            pltpu.VMEM((rows, fluxes, blocks_here, block), bf16),
            pltpu.VMEM((rows, fluxes, blocks_here, block), bf16),
            pltpu.VMEM((rows, fluxes, blocks_here, block), bf16),
            pltpu.VMEM((blocks_here * fluxes, block), f32),
            sem((blocks_here,)),
            sem,
            sem((13,)),
            sem((blocks // GROUP,)),
            sem((2,)),
            sem((3, rows, pieces)),
            sem((cells, pieces)),
            sem((rows,)),
            sem((rows,)),
            sem((rows,)),
            sem((rows,)),
        ],
        compiler_params=pltpu.CompilerParams(collective_id=0, has_side_effects=True),
    )(
        ocn_map.T,
        ocn_local.T,
        lnd_map.T,
        lnd_local.T,
        atm_fields,
        ocn_state,
        ice_state,
        ice_level.reshape(ocean_blocks, block),
        lnd_state,
        lnd_level.reshape(land_blocks, block),
        ocn_tiles,
        lnd_tiles,
    )
    return pl.pallas_call(
        finish_kernel,
        out_shape=shapes,
        in_specs=[vmem_spec] * 3,
        out_specs=(vmem_spec,) * 3,
    )(*results)


def solution(mesh):
    sects, cells = mesh.shape["sect"], mesh.shape["cell"]
    cut = ("sect", "cell")
    wide, flat = P(None, cut), P(cut)
    pair, quad = P(cut, None), P(cut, None, None, None)
    in_specs = (
        wide, wide, wide, flat, wide, flat, pair, pair, quad, pair, pair, quad,
    )
    return jax.shard_map(
        functools.partial(per_device, sects, cells),
        mesh=mesh,
        in_specs=in_specs,
        out_specs=(wide, wide, wide),
        check_vma=False,
    )
```
